256 devices in a mesh: dp: 8 (over z), tm: 32 (over y, x, core).
Axes of the slice: x: 4, y: 4, z: 8, core: 2. Of those that a mesh axis runs over, the one named last changes fastest.
Arguments:
- video: bfloat16 [8, 96, 256, 768], P('dp', 'tm'), may hold values from -6 to 6
- frame_count: int32 [8], P('dp'), may hold values from 24 to 96, as said below
- w_qkv: bfloat16 [768, 2304], replicated, may hold values from -1 to 1
- w_out: bfloat16 [768, 768], replicated, may hold values from -0.21875 to 0.21875
- cotangent: bfloat16 [8, 96, 256, 768], P('dp', 'tm'), may hold values from -6 to 6
Outputs:
- grad_video: bfloat16 [8, 96, 256, 768], P('dp', 'tm')
- grad_qkv: float32 [768, 2304], P('tm', 'dp')
- grad_out: float32 [768, 768], P('tm', 'dp')
The draws below stay inside these ranges and needn't reach their ends.
Inputs may be any that keep to these rules, and one draw needn't show every extreme that they name: `frame_count`: frames at or after a video's count are padding; some video has all 96 frames.
All inputs are finite; a program needn't handle non-finite values.
Results may differ from the reference program's by a relative error of at most 0.018.
The reference program's roundings to bfloat16 on the way count: a program that leaves them out, or rounds other values in their place, can miss the bound.
Values may be sent and summed in bfloat16 or wider, within the bound.
No kernel may reach another device: no remote copies, remote signals or barrier semaphores. Data moves between devices by JAX's collectives and lax.ppermute only.
A program may use at most 128 MiB of HBM per device.

```python
import math
import jax
import jax.numpy as jnp
from jax import lax

HEADS = 12
HEAD_DIM = 64
D = 768
PATCHES = 256
FRAMES = 96
VIDEOS = 8


def draw_video(key, part):
    key_base = jax.random.fold_in(key, 0)
    full_shape = (VIDEOS, FRAMES, PATCHES, D)
    result = jnp.clip(jax.random.normal(key_base, full_shape, jnp.float32), -6.0, 6.0)
    return result.astype(jnp.bfloat16)


def draw_frame_count(key, part):
    key_counts, key_full = jax.random.split(key, 2)
    lengths = jax.random.randint(key_counts, (VIDEOS,), max(1, FRAMES // 4), FRAMES + 1)
    fullest = jax.random.randint(key_full, (), 0, VIDEOS)
    return jnp.where(jnp.arange(VIDEOS) == fullest, FRAMES, lengths).astype(jnp.int32)


def draw_w_qkv(key, part):
    key_common = jax.random.fold_in(key, 0)
    key_noise = jax.random.fold_in(key, 2)
    key_value = jax.random.fold_in(key, 3)
    query_part = jax.random.normal(key_common, (D, D), jnp.float32) / math.sqrt(D)
    key_part = jax.random.normal(key_noise, (D, D), jnp.float32) / math.sqrt(D)
    value_part = jax.random.normal(key_value, (D, D), jnp.float32) / math.sqrt(D)
    joined = jnp.concatenate([query_part, key_part, value_part], axis=1)
    return jnp.clip(joined, -1.0, 1.0).astype(jnp.bfloat16)


def strengthened(array, stream_key, source, target, blocks, factor):
    owner, partner = [(jnp.arange(array.shape[position]) // (array.shape[position] // blocks)).reshape([-1 if axis == position else 1 for axis in range(array.ndim)]) for position in (source, target)]
    chosen = jax.random.permutation(stream_key, blocks)[partner]
    strong = (owner == chosen) | (owner == (partner + blocks // 2) % blocks)
    return jnp.where(strong, factor * array, array)


def block_levels(key, dims, cuts, smallest, high):
    def one(axis_at, shards_of):
        heights = jax.random.uniform(jax.random.fold_in(jax.random.fold_in(key, 6), axis_at), (shards_of,), jnp.float32, smallest / len(cuts), high / len(cuts))
        return jnp.repeat(jnp.exp(heights), dims[axis_at] // shards_of).reshape((-1,) + (1,) * (len(dims) - axis_at - 1))

    gain = one(*cuts[0])
    for cut in cuts[1:]:
        gain = gain * one(*cut)
    return gain


def normal_values(own_key, shape, width, bound, pieces=(), kind=jnp.bfloat16):
    entries = width * jax.random.normal(own_key, shape, jnp.float32)
    if pieces:
        entries = entries * block_levels(own_key, shape, pieces, -0.22, 0.18)
    return jnp.clip(entries, -bound, bound).astype(kind)


def gaussian_with(own_key, shape, scale, bound, cuts, heavy, held_as=jnp.bfloat16):
    drawn = scale * jax.random.normal(own_key, shape, jnp.float32)
    if cuts:
        drawn = drawn * block_levels(own_key, shape, cuts, -0.22, 0.18)
    return jnp.clip(strengthened(drawn, jax.random.fold_in(own_key, 3), *heavy), -bound, bound).astype(held_as)


def setup_inputs(seed: int = 0) -> dict:
    splits = jax.random.split(jax.random.key(seed), 6)
    video = draw_video(jax.random.fold_in(splits[5], 71), 0)
    frame_count = draw_frame_count(jax.random.fold_in(splits[5], 71), 0)
    w_qkv = draw_w_qkv(jax.random.fold_in(splits[5], 71), 0)
    w_out = normal_values(splits[3], (D, D), D ** -0.5, 0.21875)
    cotangent = gaussian_with(splits[4], (VIDEOS, FRAMES, PATCHES, D), 1.0, 6.0, ((0, 8), (1, 32)), (1, 3, 32, 2.75))
    return dict(video=video, frame_count=frame_count, w_qkv=w_qkv, w_out=w_out, cotangent=cotangent)


def normalize(tokens):
    values = tokens.astype(jnp.float32)
    centred = values - lax.optimization_barrier(jnp.mean(values, axis=-1, keepdims=True))
    inverse = lax.rsqrt(lax.optimization_barrier(jnp.mean(centred * centred, axis=-1, keepdims=True)) + 1e-05)
    return (centred * inverse, inverse)

def attend(packed, grad_attn, present, head_count, head_dim):
    frames, places = (packed.shape[0], packed.shape[1])
    model_width = head_count * head_dim
    shaped = packed.reshape(frames, places, 3, head_count, head_dim)
    query_part = shaped[:, :, 0].astype(jnp.float32)
    key_part = shaped[:, :, 1].astype(jnp.float32)
    value_part = shaped[:, :, 2].astype(jnp.float32)
    scaling = 1.0 / math.sqrt(head_dim)
    scores = jnp.einsum('fphe,gphe->phfg', query_part, key_part) * scaling
    scores = jnp.where(present[None, None, None, :], scores, -1e+30)
    row_peak = lax.optimization_barrier(jnp.max(scores, axis=-1, keepdims=True))
    raised = jnp.exp(scores - row_peak)
    weights = raised / lax.optimization_barrier(jnp.sum(raised, axis=-1, keepdims=True))
    weights_low = weights.astype(jnp.bfloat16)
    mixture = jnp.einsum('phfg,gphe->fphe', weights_low.astype(jnp.float32), value_part)
    query_mask = present.astype(jnp.float32)[:, None, None, None]
    attended = (mixture * query_mask).astype(jnp.bfloat16).reshape(frames, places, model_width)
    grad_heads = grad_attn.reshape(frames, places, head_count, head_dim)
    grad_heads = jnp.where(present[:, None, None, None], grad_heads, jnp.zeros((), jnp.bfloat16))
    grad_wide = grad_heads.astype(jnp.float32)
    grad_values = jnp.einsum('phfg,fphe->gphe', weights_low.astype(jnp.float32), grad_wide).astype(jnp.bfloat16)
    grad_weights = jnp.einsum('fphe,gphe->phfg', grad_wide, value_part)
    inner_sum = lax.optimization_barrier(jnp.sum(weights * grad_weights, axis=-1, keepdims=True))
    grad_scores = (weights * (grad_weights - inner_sum) * scaling).astype(jnp.bfloat16)
    grad_queries = jnp.einsum('phfg,gphe->fphe', grad_scores.astype(jnp.float32), key_part).astype(jnp.bfloat16)
    grad_keys = jnp.einsum('phfg,fphe->gphe', grad_scores.astype(jnp.float32), query_part).astype(jnp.bfloat16)
    grad_packed = jnp.stack([grad_queries, grad_keys, grad_values], axis=2).reshape(frames, places, 3 * model_width)
    return (attended, grad_packed)

def reference(video, frame_count, w_qkv, w_out, cotangent):
    videos, frames, patches, model_width = video.shape

    def one_video(totals, slices):
        grad_in, grad_proj = totals
        tokens, incoming, length = slices
        normed, inverse = normalize(tokens)
        hidden = normed.astype(jnp.bfloat16)
        flat_hidden = hidden.reshape(-1, model_width)
        flat_incoming = incoming.reshape(-1, model_width)
        packed = jnp.dot(flat_hidden, w_qkv, preferred_element_type=jnp.float32).astype(jnp.bfloat16)
        packed = packed.reshape(frames, patches, 3 * model_width)
        grad_attn = jnp.dot(flat_incoming, w_out.T, preferred_element_type=jnp.float32).astype(jnp.bfloat16)
        grad_attn = grad_attn.reshape(frames, patches, model_width)
        present = jnp.arange(frames, dtype=jnp.int32) < length
        attended, grad_packed = attend(packed, grad_attn, present, HEADS, HEAD_DIM)
        flat_grad = grad_packed.reshape(-1, 3 * model_width)
        grad_proj = grad_proj + jnp.dot(attended.reshape(-1, model_width).T, flat_incoming, preferred_element_type=jnp.float32)
        grad_in = grad_in + jnp.dot(flat_hidden.T, flat_grad, preferred_element_type=jnp.float32)
        grad_hidden = jnp.dot(flat_grad, w_qkv.T, preferred_element_type=jnp.float32).astype(jnp.bfloat16)
        grad_hidden = lax.optimization_barrier(grad_hidden).astype(jnp.float32).reshape(frames, patches, model_width)
        middle = lax.optimization_barrier(jnp.mean(grad_hidden, axis=-1, keepdims=True))
        projected = lax.optimization_barrier(jnp.mean(grad_hidden * normed, axis=-1, keepdims=True))
        grad_tokens = incoming.astype(jnp.float32) + inverse * (grad_hidden - middle - normed * projected)
        return ((grad_in, grad_proj), grad_tokens.astype(jnp.bfloat16))
    starting = (jnp.zeros((model_width, 3 * model_width), jnp.float32), jnp.zeros((model_width, model_width), jnp.float32))
    totals, grad_video = lax.scan(one_video, starting, (video, cotangent, frame_count))
    factor = 1.0 / math.sqrt(videos * frames * patches)
    return (grad_video, totals[0] * factor, totals[1] * factor)
```

```python
import math

import jax
import jax.numpy as jnp
from jax import lax
from jax.sharding import PartitionSpec as P

HEADS = 12
HEAD_DIM = 64
f32 = jnp.float32
bf16 = jnp.bfloat16


def normalize(tokens):
    values = tokens.astype(f32)
    centred = values - jnp.mean(values, axis=-1, keepdims=True)
    inverse = lax.rsqrt(jnp.mean(centred * centred, axis=-1, keepdims=True) + 1e-05)
    return (centred * inverse, inverse)


def attend(packed, grad_attn, present, head_count, head_dim):
    frames, places = (packed.shape[0], packed.shape[1])
    model_width = head_count * head_dim
    shaped = packed.reshape(frames, places, 3, head_count, head_dim)
    query_part = shaped[:, :, 0]
    key_part = shaped[:, :, 1]
    value_part = shaped[:, :, 2]
    scaling = 1.0 / math.sqrt(head_dim)
    scores = jnp.einsum("fphe,gphe->phfg", query_part, key_part, preferred_element_type=f32) * scaling
    scores = jnp.where(present[None, None, None, :], scores, -1e30)
    row_peak = jnp.max(scores, axis=-1, keepdims=True)
    raised = jnp.exp(scores - row_peak)
    weights = raised / jnp.sum(raised, axis=-1, keepdims=True)
    weights_low = weights.astype(bf16)
    mixture = jnp.einsum("phfg,gphe->fphe", weights_low, value_part, preferred_element_type=f32)
    query_mask = present.astype(f32)[:, None, None, None]
    attended = (mixture * query_mask).astype(bf16).reshape(frames, places, model_width)
    grad_heads = grad_attn.reshape(frames, places, head_count, head_dim)
    grad_heads = jnp.where(present[:, None, None, None], grad_heads, jnp.zeros((), bf16))
    grad_values = jnp.einsum("phfg,fphe->gphe", weights_low, grad_heads, preferred_element_type=f32).astype(bf16)
    grad_weights = jnp.einsum("fphe,gphe->phfg", grad_heads, value_part, preferred_element_type=f32)
    inner_sum = jnp.sum(weights * grad_weights, axis=-1, keepdims=True)
    grad_scores = (weights * (grad_weights - inner_sum) * scaling).astype(bf16)
    grad_queries = jnp.einsum("phfg,gphe->fphe", grad_scores, key_part, preferred_element_type=f32).astype(bf16)
    grad_keys = jnp.einsum("phfg,fphe->gphe", grad_scores, query_part, preferred_element_type=f32).astype(bf16)
    grad_packed = jnp.stack([grad_queries, grad_keys, grad_values], axis=2).reshape(
        frames, places, 3 * model_width
    )
    return (attended, grad_packed)


def gather_sum(pieces, axis, position, size, pairs_of):
    total = lax.dynamic_index_in_dim(pieces, position, 0, keepdims=False).astype(f32)
    arrived = []
    for shift in range(1, size):
        piece = lax.dynamic_index_in_dim(pieces, (position + shift) % size, 0, keepdims=False)
        arrived.append(lax.ppermute(piece, axis, pairs_of(shift)))
    for part in arrived:
        total = total + part.astype(f32)
    return total


def along(size, stride):
    def pairs_of(shift):
        pairs = []
        for place in range(32):
            digit = (place // stride) % size
            pairs.append((place, place + ((digit + shift) % size - digit) * stride))
        return pairs

    return pairs_of


def reduce_weights(partial):
    place = lax.axis_index("tm")
    y, x, core = place // 8, (place // 2) % 4, place % 2
    rows = partial.reshape(4, 4, 2, 24, 3072)
    own = lax.dynamic_index_in_dim(rows, core, 2, keepdims=False)
    give = lax.dynamic_index_in_dim(rows, 1 - core, 2, keepdims=False)
    chip = (own.astype(f32) + lax.ppermute(give, "tm", along(2, 1)(1)).astype(f32)).astype(bf16)
    first = chip[..., :1536]
    second = chip[..., 1536:]
    first = gather_sum(jnp.swapaxes(first, 0, 1), "tm", x, 4, along(4, 2)).astype(bf16)
    second = gather_sum(second, "tm", y, 4, along(4, 8)).astype(bf16)
    first = gather_sum(first, "tm", y, 4, along(4, 8)).astype(bf16)
    second = gather_sum(second, "tm", x, 4, along(4, 2)).astype(bf16)
    both = jnp.concatenate([first, second], axis=1)
    parts = both.reshape(24, 8, 384).transpose(1, 0, 2)
    parts = lax.all_to_all(parts, "dp", split_axis=0, concat_axis=0, tiled=True)
    return jnp.sum(parts.astype(f32), axis=0)


def per_device(video, frame_count, w_qkv, w_out, cotangent):
    length = frame_count[0]
    local_frames, patches, model_width = video.shape[1:]
    time_devices = lax.axis_size("tm")
    data_devices = lax.axis_size("dp")
    frames = local_frames * time_devices
    places = patches // time_devices
    tokens = lax.all_to_all(video[0], "tm", split_axis=1, concat_axis=0, tiled=True)
    incoming = lax.all_to_all(cotangent[0], "tm", split_axis=1, concat_axis=0, tiled=True)
    normed, inverse = normalize(tokens)
    hidden = normed.astype(bf16)
    present = lax.iota(jnp.int32, frames) < length
    contract_rows = (((0,), (0,)), ((), ()))
    contract_cols = (((1,), (1,)), ((), ()))
    flat_hidden = hidden.reshape(-1, model_width)
    flat_incoming = incoming.reshape(-1, model_width)
    packed = jnp.dot(flat_hidden, w_qkv, preferred_element_type=f32).astype(bf16)
    packed = packed.reshape(frames, places, 3 * model_width)
    grad_attn = lax.dot_general(flat_incoming, w_out, contract_cols, preferred_element_type=f32).astype(bf16)
    grad_attn = grad_attn.reshape(frames, places, model_width)
    attended, grad_packed = attend(packed, grad_attn, present, HEADS, HEAD_DIM)
    flat_grad = grad_packed.reshape(-1, 3 * model_width)
    grad_proj = lax.dot_general(
        attended.reshape(-1, model_width), flat_incoming, contract_rows, preferred_element_type=f32
    )
    grad_in = lax.dot_general(flat_hidden, flat_grad, contract_rows, preferred_element_type=f32)
    grad_hidden = lax.dot_general(flat_grad, w_qkv, contract_cols, preferred_element_type=f32).astype(bf16)
    grad_hidden = grad_hidden.reshape(frames, places, model_width)
    grad_hidden = lax.optimization_barrier(grad_hidden).astype(f32)
    middle = jnp.mean(grad_hidden, axis=-1, keepdims=True)
    projected = jnp.mean(grad_hidden * normed, axis=-1, keepdims=True)
    grad_tokens = incoming.astype(f32) + inverse * (grad_hidden - middle - normed * projected)
    grad_tokens = lax.all_to_all(grad_tokens.astype(bf16), "tm", split_axis=0, concat_axis=1, tiled=True)
    factor = 1.0 / math.sqrt(data_devices * frames * patches)
    partial = jnp.concatenate(
        [grad_in.astype(bf16).reshape(768, 8, 288), grad_proj.astype(bf16).reshape(768, 8, 96)], axis=2
    ).reshape(768, 3072)
    total = reduce_weights(partial) * factor
    return (grad_tokens[None], total[:, :288], total[:, 288:])


def solution(mesh):
    placed = (P("dp", "tm", None, None), P("dp"), P(), P(), P("dp", "tm", None, None))
    return jax.shard_map(
        per_device,
        mesh=mesh,
        in_specs=placed,
        out_specs=(P("dp", "tm", None, None), P("tm", "dp"), P("tm", "dp")),
        check_vma=False,
    )
```

```python
import math

import jax
import jax.numpy as jnp
from jax import lax
from jax.experimental import pallas as pl
from jax.experimental.pallas import tpu as pltpu
from jax.sharding import PartitionSpec as P

HEADS = 12
HEAD_DIM = 64
D = 768
FRAMES = 96
PLACES = 8
TOKENS = FRAMES * PLACES
PAIRS = HEADS // 2
PAIR = 2 * HEAD_DIM
EPS = 1e-05
f32 = jnp.float32
bf16 = jnp.bfloat16
ROWS = (((0,), (0,)), ((), ()))
COLS = (((1,), (1,)), ((), ()))
VMEM = pl.BlockSpec(memory_space=pltpu.VMEM)


def dot(a, b, dims=(((1,), (0,)), ((), ()))):
    return lax.dot_general(a, b, dims, preferred_element_type=f32)


def statistics(values):
    centred = values - jnp.mean(values, axis=-1, keepdims=True)
    inverse = lax.rsqrt(jnp.mean(centred * centred, axis=-1, keepdims=True) + EPS)
    return centred * inverse, inverse


def rows_of(place):
    return pl.ds(place * FRAMES, FRAMES)


def spread(wide, values):
    for slab in range(D // 128):
        wide[slab] = values[:, slab * 128 : (slab + 1) * 128]


def frames_of(wide, place):
    rows = pl.ds(place, FRAMES, stride=PLACES)
    return jnp.concatenate([wide[slab, rows, :] for slab in range(D // 128)], axis=1)


def normalize_kernel(x_ref, sorted_ref, hidden_ref, wide):
    spread(wide, x_ref[...].astype(f32))
    for place in range(PLACES):
        values = frames_of(wide, place)
        sorted_ref[rows_of(place), :] = values.astype(bf16)
        hidden_ref[rows_of(place), :] = statistics(values)[0].astype(bf16)


def sort_kernel(x_ref, sorted_ref, wide):
    spread(wide, x_ref[...].astype(f32))
    for place in range(PLACES):
        sorted_ref[rows_of(place), :] = frames_of(wide, place).astype(bf16)


def finish_kernel(grad_ref, x_ref, incoming_ref, out_ref, wide):
    for place in range(PLACES):
        rows = rows_of(place)
        normed, inverse = statistics(x_ref[rows, :].astype(f32))
        grad = grad_ref[rows, :].astype(f32)
        middle = jnp.mean(grad, axis=-1, keepdims=True)
        projected = jnp.mean(grad * normed, axis=-1, keepdims=True)
        total = incoming_ref[rows, :].astype(f32) + inverse * (grad - middle - normed * projected)
        for slab in range(D // 128):
            wide[slab, pl.ds(place, FRAMES, stride=PLACES), :] = total[:, slab * 128 : (slab + 1) * 128]
    for slab in range(D // 128):
        out_ref[:, slab * 128 : (slab + 1) * 128] = wide[slab].astype(bf16)


def stacked(pair, low):
    zero = jnp.zeros_like(pair)
    return jnp.concatenate([jnp.where(low, pair, zero), jnp.where(low, zero, pair)], axis=0)


def chosen(both, low):
    return jnp.where(low, both[:FRAMES], both[FRAMES:])


def forward_kernel(length_ref, packed_ref, attended_ref, weights_ref):
    length = length_ref[0]
    low = lax.broadcasted_iota(jnp.int32, (FRAMES, PAIR), 1) < HEAD_DIM
    real_key = lax.broadcasted_iota(jnp.int32, (2, FRAMES, FRAMES), 1) < length
    real_row = lax.broadcasted_iota(jnp.int32, (FRAMES, PAIR), 0) < length
    scaling = 1.0 / math.sqrt(HEAD_DIM)
    for pair in range(PAIRS):
        at = pair * PAIR
        query = packed_ref[:, at : at + PAIR]
        key = packed_ref[:, D + at : D + at + PAIR]
        value = packed_ref[:, 2 * D + at : 2 * D + at + PAIR]
        scores = dot(stacked(key, low), query, COLS) * scaling
        scores = jnp.where(real_key, scores.reshape(2, FRAMES, FRAMES), -1e30)
        raised = jnp.exp(scores - jnp.max(scores, axis=1, keepdims=True))
        weights = raised / jnp.sum(raised, axis=1, keepdims=True)
        weights = weights.reshape(2 * FRAMES, FRAMES)
        weights_ref[pair * 2 * FRAMES : (pair + 1) * 2 * FRAMES, :] = weights
        mixture = dot(weights.astype(bf16), stacked(value, low), ROWS)
        attended_ref[:, at : at + PAIR] = jnp.where(real_row, mixture, 0.0).astype(bf16)


def backward_kernel(length_ref, packed_ref, weights_ref, grad_ref, out_ref):
    length = length_ref[0]
    low = lax.broadcasted_iota(jnp.int32, (FRAMES, PAIR), 1) < HEAD_DIM
    real_row = lax.broadcasted_iota(jnp.int32, (FRAMES, PAIR), 0) < length
    scaling = 1.0 / math.sqrt(HEAD_DIM)
    for pair in range(PAIRS):
        at = pair * PAIR
        query = packed_ref[:, at : at + PAIR]
        key = packed_ref[:, D + at : D + at + PAIR]
        value = packed_ref[:, 2 * D + at : 2 * D + at + PAIR]
        grad = grad_ref[:, at : at + PAIR]
        grad = jnp.where(real_row, grad, jnp.zeros_like(grad))
        weights = weights_ref[pair * 2 * FRAMES : (pair + 1) * 2 * FRAMES, :]
        grad_value = dot(weights.astype(bf16), grad)
        grad_weights = dot(stacked(value, low), grad, COLS)
        inner = jnp.sum((weights * grad_weights).reshape(2, FRAMES, FRAMES), axis=1, keepdims=True)
        weights = weights.reshape(2, FRAMES, FRAMES)
        grad_weights = grad_weights.reshape(2, FRAMES, FRAMES)
        grad_scores = (weights * (grad_weights - inner) * scaling).astype(bf16)
        grad_scores = grad_scores.reshape(2 * FRAMES, FRAMES)
        grad_query = dot(grad_scores, stacked(key, low), ROWS)
        grad_key = dot(grad_scores, query)
        out_ref[:, at : at + PAIR] = grad_query.astype(bf16)
        out_ref[:, D + at : D + at + PAIR] = chosen(grad_key, low).astype(bf16)
        out_ref[:, 2 * D + at : 2 * D + at + PAIR] = chosen(grad_value, low).astype(bf16)


def whole(kernel, outs, scratch, *args):
    return pl.pallas_call(
        kernel,
        out_shape=outs,
        in_specs=[VMEM] * len(args),
        out_specs=[VMEM] * len(outs),
        scratch_shapes=scratch,
    )(*args)


def per_place(width):
    return pl.BlockSpec((FRAMES, width), lambda place, length: (place, 0))


WEIGHTS = pl.BlockSpec((PAIRS * 2 * FRAMES, FRAMES), lambda place, length: (place, 0))


def attention(kernel, length, ins, in_specs, outs, out_specs):
    return pl.pallas_call(
        kernel,
        out_shape=outs,
        grid_spec=pltpu.PrefetchScalarGridSpec(
            num_scalar_prefetch=1, grid=(PLACES,), in_specs=in_specs, out_specs=out_specs
        ),
    )(length, *ins)


def shape(rows, width, kind=bf16):
    return jax.ShapeDtypeStruct((rows, width), kind)


def along(size, stride):
    def pairs_of(shift):
        pairs = []
        for place in range(32):
            digit = (place // stride) % size
            pairs.append((place, place + ((digit + shift) % size - digit) * stride))
        return pairs

    return pairs_of


def gather_sum(pieces, position, size, pairs_of):
    total = lax.dynamic_index_in_dim(pieces, position, 0, keepdims=False).astype(f32)
    arrived = []
    for shift in range(1, size):
        piece = lax.dynamic_index_in_dim(pieces, (position + shift) % size, 0, keepdims=False)
        arrived.append(lax.ppermute(piece, "tm", pairs_of(shift)))
    for part in arrived:
        total = total + part.astype(f32)
    return total


def exchange(blocks):
    return lax.all_to_all(blocks, "tm", split_axis=0, concat_axis=0, tiled=True)


def to_places(local):
    blocks = local.reshape(-1, FRAMES // 3, PLACES, D).transpose(1, 0, 2, 3)
    return exchange(blocks.reshape(FRAMES // 3, -1, D)).reshape(TOKENS, D)


def to_frames(tokens):
    blocks = exchange(tokens.reshape(FRAMES // 3, -1, D)).reshape(FRAMES // 3, -1, PLACES, D)
    return blocks.transpose(1, 0, 2, 3).reshape(-1, PLACES * FRAMES // 3, D)


def columns(core, x_first):
    at = lax.iota(jnp.int32, D // 2)
    major, minor, row = at // 96, (at // 24) % 4, at % 24
    y, x = (minor, major) if x_first else (major, minor)
    feature = ((y * 4 + x) * 2 + core) * 24 + row
    return (lax.broadcasted_iota(jnp.int32, (D // 2, D), 1) == feature[:, None]).astype(bf16)


def per_device(video, frame_count, w_qkv, w_out, cotangent):
    local_frames, patches, width = video.shape[1:]
    length = frame_count
    place = lax.axis_index("tm")
    y, x, core = place // 8, (place // 2) % 4, place % 2
    factor = 1.0 / math.sqrt(lax.axis_size("dp") * FRAMES * patches)

    tokens = to_places(video[0])
    incoming = to_places(cotangent[0])

    scratch = [pltpu.VMEM((D // 128, TOKENS, 128), f32)]
    small = shape(TOKENS, D)
    tokens, hidden = whole(normalize_kernel, [small, small], scratch, tokens)
    packed = dot(hidden, w_qkv).astype(bf16)
    attended, weights = attention(
        forward_kernel,
        length,
        [packed],
        [per_place(3 * D)],
        [small, shape(PLACES * PAIRS * 2 * FRAMES, FRAMES, f32)],
        [per_place(D), WEIGHTS],
    )
    picks = [(columns(c, True), columns(c, False)) for c in (1 - core, core)]
    lefts = [
        tuple(dot(pick, side, COLS).astype(bf16) for pick, side in ((a, hidden), (b, hidden), (b, attended)))
        for a, b in picks
    ]
    lefts, incoming, packed, weights = lax.optimization_barrier((lefts, incoming, packed, weights))

    (incoming,) = whole(sort_kernel, [small], scratch, incoming)
    grad_attn = dot(incoming, w_out, COLS).astype(bf16)
    (grad_packed,) = attention(
        backward_kernel,
        length,
        [packed, weights, grad_attn],
        [per_place(3 * D), WEIGHTS, per_place(D)],
        [shape(TOKENS, 3 * D)],
        [per_place(3 * D)],
    )

    cut = 2 * D
    rights = (grad_packed[:, :cut], grad_packed[:, cut:], incoming)
    gives = [dot(l, r).astype(bf16) for l, r in zip(lefts[0], rights)]
    gives, later = lax.optimization_barrier((gives, grad_packed))
    got = [lax.ppermute(g, "tm", along(2, 1)(1)) for g in gives]
    owns = [dot(l, r) for l, r in zip(lefts[1], rights)]
    sums = [(o + g.astype(f32)).astype(bf16) for o, g in zip(owns, got)]
    first = sums[0].reshape(4, 96, cut)
    second = jnp.concatenate(sums[1:], axis=1).reshape(4, 96, cut)
    over_x, over_y = along(4, 2), along(4, 8)
    first = gather_sum(first, x, 4, over_x).astype(bf16)
    second = gather_sum(second, y, 4, over_y).astype(bf16)
    first = gather_sum(first.reshape(4, 24, cut), y, 4, over_y).astype(bf16)
    second = gather_sum(second.reshape(4, 24, cut), x, 4, over_x).astype(bf16)
    whole_rows = jnp.concatenate([first, second], axis=1)
    parts = jnp.concatenate(
        [whole_rows[:, : 3 * D].reshape(24, 8, 288), whole_rows[:, 3 * D :].reshape(24, 8, 96)], axis=2
    ).transpose(1, 0, 2)
    parts = lax.all_to_all(parts, "dp", split_axis=0, concat_axis=0, tiled=True)
    total = jnp.sum(parts.astype(f32), axis=0) * factor

    grad_hidden = dot(later, w_qkv, COLS).astype(bf16)
    (grad_tokens,) = whole(finish_kernel, [small], scratch, grad_hidden, tokens, incoming)
    return (to_frames(grad_tokens)[None], total[:, :288], total[:, 288:])


def solution(mesh):
    placed = (P("dp", "tm", None, None), P("dp"), P(), P(), P("dp", "tm", None, None))
    return jax.shard_map(
        per_device,
        mesh=mesh,
        in_specs=placed,
        out_specs=(P("dp", "tm", None, None), P("tm", "dp"), P("tm", "dp")),
        check_vma=False,
    )
```
